256 devices in a mesh: row: 8 (over x, y_hi), col: 32 (over z, y_lo, core).
Axes of the slice: x: 4, y: 4 (y_hi: 2, y_lo: 2; y = y_hi * 2 + y_lo), z: 8, core: 2. Of those that a mesh axis runs over, the one named last changes fastest.
Arguments:
- design: bfloat16 [2048, 24576], P('row', 'col'), may hold values from -6 to 6
- observations: bfloat16 [2048], P('row'), may hold values from -6 to 6
- filter_taps: float32 [64], replicated, may hold values from -0.5 to 0.5
- tap_count: int32 [4], replicated, may hold values from 32 to 64
- arc_id: int32 [2048], replicated, may hold values from 0 to 3, never falling along the last dimension, each value on 1 to 1024 neighbouring positions
Outputs:
- normal: float32 [24576, 24576], P('row', 'col')
- right_side: float32 [24576], P('col')
The draws below stay inside these ranges and needn't reach their ends.
Inputs may be any that keep to these rules, and one draw needn't show every extreme that they name: `arc_id`: arc numbers never fall along the epochs; every arc holds 1 to 1024 epochs and one holds exactly 1024.
All inputs are finite; a program needn't handle non-finite values.
Results may differ from the reference program's by a relative error of at most 0.0031.
Values may be sent and summed in bfloat16 or wider, within the bound.
A program may use at most 128 MiB of HBM per device.

```python
import math
import jax
import jax.numpy as jnp
import numpy as np
from jax import lax

P_SIZE = 24576
K = 64
ARCS = 4
EPOCHS = 2048
ARC_MOST = 1024


def touch_ends(drawn, rng, low, top_value):
    shape = drawn.shape
    spot = [jax.random.randint(jax.random.fold_in(rng, axis), (), 0, shape[axis]) for axis in range(len(shape))]
    drawn = drawn.at[tuple(spot)].set(low)
    longest = shape.index(max(shape))
    spot[longest] = (spot[longest] + 1) % shape[longest]
    return drawn.at[tuple(spot)].set(top_value)


def block_scale(key, extent, split, smallest, high):
    gain = 1.0
    for position, parts in split:
        heights = jax.random.uniform(jax.random.fold_in(jax.random.fold_in(key, 6), position), (parts,), jnp.float32, smallest / len(split), high / len(split))
        gain = gain * jnp.repeat(jnp.exp(heights), extent[position] // parts).reshape((-1,) + (1,) * (len(extent) - 1 - position))
    return gain


def split_up(count, total, most, lean):
    loads = [(1 << 20) // math.isqrt(rank ** lean) + 1 for rank in range(2, count + 1)]
    surplus, given = total - most - (count - 1), [1] * (count - 1)
    while surplus > 0:
        candidates = [i for i in range(count - 1) if given[i] < most]
        whole, remaining = sum([loads[i] for i in candidates]), surplus
        for i in candidates:
            addition = min(most - given[i], max(1, remaining * loads[i] // whole), surplus)
            given[i] = given[i] + addition
            surplus = surplus - addition
    return np.array([most] + given)


def ragged(key, count, total, bound, slope):
    if count == 2:
        one = jax.random.randint(key, (), max(1, total - bound), min(bound, total - 1) + 1)
        return jnp.stack([one, total - one])
    sizes = jnp.asarray(split_up(count, total, bound, slope), jnp.int32)
    pairs = (count - 1) // 2
    giver, receiver = sizes[1:1 + 2 * pairs:2], sizes[2:2 + 2 * pairs:2]
    room = jnp.minimum(giver - 1, bound - receiver)
    moved = jax.random.randint(jax.random.fold_in(key, 1), (pairs,), 0, 1 << 20) % (room + 1)
    sizes = sizes.at[1:1 + 2 * pairs:2].set(giver - moved).at[2:2 + 2 * pairs:2].set(receiver + moved)
    return sizes[jax.random.permutation(jax.random.fold_in(key, 2), count)]


def normal_values(rng, dims, width, bound, cuts=(), held_as=jnp.bfloat16):
    result = jax.random.normal(rng, dims, jnp.float32) * width
    if len(cuts) > 0:
        result = block_scale(rng, dims, cuts, -0.22, 0.18) * result
    return jnp.clip(result, min=-bound, max=bound).astype(held_as)


def setup_inputs(seed: int = 0) -> dict:
    streams_of = jax.random.split(jax.random.key(seed), 6)
    design = normal_values(streams_of[0], (EPOCHS, P_SIZE), 1.0, 6.0, ((0, 8), (1, 32)))
    observations = normal_values(streams_of[1], (EPOCHS,), 1.0, 6.0, ((0, 8),))
    filter_taps = normal_values(streams_of[2], (K,), 0.125, 0.5, (), jnp.float32)
    tap_count = touch_ends(jax.random.randint(streams_of[3], (ARCS,), K // 2, K + 1), jax.random.fold_in(streams_of[3], 1), K // 2, K).astype(jnp.int32)
    arc_id = jnp.searchsorted(jnp.cumsum(ragged(streams_of[4], ARCS, EPOCHS, ARC_MOST, 0)), jnp.arange(EPOCHS), side="right").astype(jnp.int32)
    return dict(design=design, observations=observations, filter_taps=filter_taps, tap_count=tap_count, arc_id=arc_id)


def reference(design, observations, filter_taps, tap_count, arc_id):
    epoch_index = jnp.arange(EPOCHS, dtype=jnp.int32)
    lag_matrix = epoch_index[:, None] - epoch_index[None, :]
    arc_taps = tap_count[arc_id.astype(jnp.int32)].astype(jnp.int32)
    valid_lag = (lag_matrix >= 0) & (lag_matrix < K) & (lag_matrix < arc_taps[:, None])
    valid_lag = valid_lag & (arc_id[:, None] == arc_id[None, :])
    filter_rows = jnp.where(valid_lag, filter_taps[jnp.clip(lag_matrix, 0, K - 1)], jnp.float32(0.0))
    whitened = jnp.dot(filter_rows, design.astype(jnp.float32), precision=lax.Precision.HIGHEST).astype(jnp.bfloat16)
    white_obs = jnp.dot(filter_rows, observations.astype(jnp.float32), precision=lax.Precision.HIGHEST).astype(jnp.bfloat16)
    white_float = whitened.astype(jnp.float32)
    normal = jnp.dot(white_float.T, white_float, precision=lax.Precision.HIGHEST) / EPOCHS
    right_side = jnp.dot(white_obs.astype(jnp.float32), white_float, precision=lax.Precision.HIGHEST) / math.sqrt(EPOCHS)
    return (normal, right_side)
```

```python
import functools
import math

import jax
import jax.numpy as jnp
from jax import lax
from jax.experimental import pallas as pl
from jax.experimental.pallas import tpu as pltpu
from jax.sharding import Mesh
from jax.sharding import PartitionSpec as P

MESH = pl.DeviceIdType.MESH
AXES = ("x", "yh", "z", "yl", "core")
NX, NZ = 4, 8
ROWS = 8
EXTRA = 16
UP, DOWN = 0, 1


def body(
    design_ref, obs_ref, taps_ref, count_ref, arc_ref,
    out_ref, right_ref,
    cols, panel, parts, halo, halo_obs, obs_own, taps_pad,
    halo_send, halo_recv, part_send, part_recv, own_sem, panel_send, panel_recv,
    col_send, col_recv, z_send, z_recv, lo_send, lo_recv, pair_send, pair_recv,
):
    x, yh, z = lax.axis_index("x"), lax.axis_index("yh"), lax.axis_index("z")
    yl, core = lax.axis_index("yl"), lax.axis_index("core")
    row = x * 2 + yh
    mine = yl * 2 + core
    here, width = design_ref.shape
    taps = taps_ref.shape[1]
    part = width // NZ
    deep = here * ROWS
    half = deep // 2
    quarter = deep // 4

    def at_row(r):
        return {"x": r // 2, "yh": lax.rem(r, 2)}

    barrier = pltpu.get_barrier_semaphore()
    peers = [at_row(lax.rem(row + i, ROWS)) for i in range(1, ROWS)]
    peers += [{"z": lax.rem(z + i, NZ)} for i in range(1, NZ)]
    peers += [{"yl": 1 - yl}, {"core": 1 - core}]
    for peer in peers:
        pl.semaphore_signal(barrier, inc=1, device_id=peer, device_id_type=MESH)

    obs_own[...] = jnp.broadcast_to(obs_ref[...].astype(jnp.float32), obs_own.shape).astype(jnp.bfloat16)
    halo[0:taps, :] = jnp.zeros((taps, width), jnp.bfloat16)
    pl.semaphore_wait(barrier, len(peers))

    started = []

    def send(src, dst, send_sem, recv_sem, device):
        copy = pltpu.make_async_remote_copy(
            src_ref=src, dst_ref=dst, send_sem=send_sem, recv_sem=recv_sem,
            device_id=device, device_id_type=MESH,
        )
        copy.start()
        started.append(copy)

    def arrived(dst, sem):
        pltpu.make_async_copy(dst, dst, sem).wait()

    after = at_row(lax.rem(row + 1, ROWS))
    send(design_ref.at[here - taps : here, :], halo.at[taps : 2 * taps, :], halo_send.at[0], halo_recv.at[0], after)
    send(obs_own, halo_obs, halo_send.at[1], halo_recv.at[1], after)

    taps_pad[...] = jnp.zeros(taps_pad.shape, jnp.float32)
    taps_pad[0:1, 0:taps] = taps_ref[...]
    line = jnp.broadcast_to(taps_pad[0:1, :], (here, here))
    toeplitz = pltpu.roll(line, 0, 1, stride=1, stride_axis=0).T
    target = lax.broadcasted_iota(jnp.int32, (here, here), 0)
    source = lax.broadcasted_iota(jnp.int32, (here, here), 1)
    lag = target - source
    own = lag >= 0
    lag = jnp.where(own, lag, lag + here)
    arc_here = jnp.broadcast_to(arc_ref[pl.ds(row, 1), :], (here, here))
    arc_before = jnp.broadcast_to(arc_ref[pl.ds(jnp.maximum(row - 1, 0), 1), :], (here, here))
    arc_before = jnp.where(row > 0, arc_before, -1)
    arc_target = arc_here.T
    arc_source = jnp.where(own, arc_here, arc_before)
    limit = jnp.zeros((here, here), jnp.int32)
    for a in range(count_ref.shape[0]):
        limit = jnp.where(arc_target == a, count_ref[a], limit)
    rows_f = jnp.where((arc_target == arc_source) & (lag < limit) & (lag < taps), toeplitz, 0.0)

    def three(value):
        high = value.astype(jnp.bfloat16)
        rest = value - high.astype(jnp.float32)
        middle = rest.astype(jnp.bfloat16)
        return high, middle, (rest - middle.astype(jnp.float32)).astype(jnp.bfloat16)

    own_terms = three(jnp.where(own, rows_f, 0.0))
    halo_terms = three(jnp.where(own, 0.0, rows_f)[0 : 2 * taps, here - 2 * taps :])
    by_lane = (((1,), (1,)), ((), ()))

    def total(terms, value):
        return sum(jnp.dot(t, value, preferred_element_type=jnp.float32) for t in terms[::-1])

    def total_lanes(terms, value):
        return sum(
            lax.dot_general(value, t, by_lane, preferred_element_type=jnp.float32) for t in terms[::-1]
        )

    white = total(own_terms, design_ref[...])
    white_obs = total_lanes(own_terms, obs_own[...])
    arrived(halo.at[taps : 2 * taps, :], halo_recv.at[0])
    arrived(halo_obs, halo_recv.at[1])
    first = white[0 : 2 * taps] + total(halo_terms, halo[...])
    obs_first = white_obs[:, 0 : 2 * taps] + total_lanes(halo_terms, halo_obs[:, here - 2 * taps :])
    white = jnp.concatenate([first, white[2 * taps :]], axis=0).T
    white_obs = jnp.concatenate([obs_first, white_obs[:, 2 * taps :]], axis=1)
    mine_lanes = pl.ds(pl.multiple_of(row * here, here), here)
    cols[0:width, mine_lanes] = white.astype(jnp.bfloat16)
    cols[width : width + EXTRA, mine_lanes] = white_obs.astype(jnp.bfloat16)

    def shard(r):
        return cols.at[:, pl.ds(pl.multiple_of(r * here, here), here)]

    def own_part(q):
        return cols.at[pl.ds(pl.multiple_of(q * part, part), part), mine_lanes]

    near_first = [1, 7, 2, 6, 3, 5, 4]
    for i in near_first:
        q = lax.rem(z + i, NZ)
        send(own_part(q), parts.at[z], part_send.at[i], part_recv.at[i], {"z": q})
    own_copy = pltpu.make_async_copy(own_part(z), parts.at[z], part_recv.at[0])
    own_copy.start()

    right_x, left_x = lax.rem(x + 1, NX), lax.rem(x + NX - 1, NX)
    far_x = lax.rem(x + 2, NX)
    partner = x * 2 + 1 - yh
    send(shard(row), shard(row), col_send.at[0], col_recv.at[0], {"yh": 1 - yh})
    send(shard(row), shard(row), col_send.at[1], col_recv.at[1], {"x": right_x})
    send(shard(row), shard(row), col_send.at[2], col_recv.at[2], {"x": left_x})

    conditional = []
    for i in [0] + near_first:
        owner = lax.rem(z + NZ - i, NZ)
        arrived(parts.at[owner], part_recv.at[i])
        target_ref = panel.at[z, mine, :, mine_lanes]
        away = pltpu.make_async_remote_copy(
            src_ref=parts.at[owner], dst_ref=target_ref, send_sem=panel_send.at[i],
            recv_sem=panel_recv.at[row], device_id=at_row(owner), device_id_type=MESH,
        )
        local = pltpu.make_async_copy(parts.at[owner], target_ref, panel_recv.at[row])

        @pl.when(owner != row)
        def _():
            away.start()

        @pl.when(owner == row)
        def _():
            local.start()

        conditional.append((owner, away))

    arrived(shard(partner), col_recv.at[0])
    send(shard(partner), shard(partner), col_send.at[3], col_recv.at[3], {"x": right_x})
    send(shard(partner), shard(partner), col_send.at[4], col_recv.at[4], {"x": left_x})
    from_left = left_x * 2 + yh
    arrived(shard(from_left), col_recv.at[1])
    send(shard(from_left), shard(from_left), col_send.at[5], col_recv.at[5], {"x": right_x})

    F, H = 0, 1
    above, below = {"z": lax.rem(z + 1, NZ)}, {"z": lax.rem(z + NZ - 1, NZ)}
    z_device = (above, below)

    def piece(q, other, h):
        line_of = 1 - yl if other else yl
        return panel.at[q, line_of * 2 + core, :, h * half : (h + 1) * half]

    def halves(q, side):
        start = half + side * quarter
        return panel.at[q, mine, :, start : start + quarter]

    def pass_z(ref, way, d, kind):
        send(ref, ref, z_send.at[way, d, kind], z_recv.at[way, d, kind], z_device[way])

    def pass_lo(ref, slot):
        send(ref, ref, lo_send.at[slot], lo_recv.at[slot], {"yl": 1 - yl})

    def pass_pair(q, o, other, h):
        ref = piece(q, other, h)
        send(ref, ref, pair_send.at[o, other, h], pair_recv.at[o, other, h], {"core": 1 - core})

    def panel_arrived(e):
        arrived(panel.at[z, mine, :, e * here : (e + 1) * here], panel_recv.at[e])

    def group(o):
        q = lax.rem(z + NZ - o, NZ)
        for other in (0, 1):
            for h in (F, H):
                line_of = 1 - yl if other else yl
                arrived(
                    panel.at[q, line_of * 2 + 1 - core, :, h * half : (h + 1) * half],
                    pair_recv.at[o, other, h],
                )
        tile = width // 3

        @pl.loop(0, 3)
        def _(n):
            lanes = pl.ds(pl.multiple_of(n * tile, tile), tile)
            result = lax.dot_general(
                panel[q].reshape(4 * part, deep), cols[lanes, :], by_lane,
                preferred_element_type=jnp.float32,
            )
            out_ref[:, q, :, lanes] = result.reshape(4, part, tile) * (1.0 / deep)

    for e in range(4):
        panel_arrived(e)
    own_f = piece(z, 0, F)
    pass_lo(own_f, NZ)
    pass_z(own_f, UP, 1, 0)
    pass_z(own_f, DOWN, 1, 0)
    pass_pair(z, 0, 0, F)
    for e in range(4, 8):
        panel_arrived(e)
    own_h = piece(z, 0, H)
    pass_z(own_h, UP, 1, 1)
    pass_z(own_h, DOWN, 1, 1)
    pass_lo(own_h, 0)
    pass_pair(z, 0, 0, H)
    other_f = piece(z, 1, F)
    arrived(other_f, lo_recv.at[NZ])
    pass_z(other_f, UP, 1, 2)
    pass_z(other_f, DOWN, 1, 2)
    pass_pair(z, 0, 1, F)

    from_right = right_x * 2 + 1 - yh
    arrived(shard(from_right), col_recv.at[4])
    send(shard(from_right), shard(from_right), col_send.at[6], col_recv.at[6], {"x": left_x})

    def lo_arrived(o):
        q = lax.rem(z + NZ - o, NZ)
        arrived(piece(q, 1, H), lo_recv.at[o])
        pass_pair(q, o, 1, H)

    lo_arrived(0)
    kinds = ((0, F), (0, H), (1, F))

    def hop(d):
        for kind, (other, h) in enumerate(kinds):
            for way in (UP, DOWN):
                o = d if way == UP else NZ - d
                q = lax.rem(z + NZ - o, NZ)
                ref = piece(q, other, h)
                arrived(ref, z_recv.at[way, d, kind])
                if d < 3:
                    pass_z(ref, way, d + 1, kind)
                elif kind == 1:
                    pass_z(halves(q, way), way, d + 1, kind)
                elif kind == (0 if way == UP else 2):
                    pass_z(ref, way, d + 1, kind)
                if kind == 1:
                    pass_lo(ref, o)
                pass_pair(q, o, other, h)
        lo_arrived(d)
        lo_arrived(NZ - d)

    hop(1)
    hop(2)
    arrived(shard(left_x * 2 + 1 - yh), col_recv.at[3])
    arrived(shard(right_x * 2 + yh), col_recv.at[2])
    arrived(shard(far_x * 2 + yh), col_recv.at[5])
    arrived(shard(far_x * 2 + 1 - yh), col_recv.at[6])
    group(0)
    hop(3)
    group(1)
    group(7)
    far = lax.rem(z + 4, NZ)
    for way in (UP, DOWN):
        arrived(halves(far, way), z_recv.at[way, 4, 1])
    pass_lo(piece(far, 0, H), 4)
    pass_pair(far, 4, 0, H)
    group(2)
    group(6)
    arrived(piece(far, 0, F), z_recv.at[UP, 4, 0])
    pass_pair(far, 4, 0, F)
    arrived(piece(far, 1, F), z_recv.at[DOWN, 4, 2])
    pass_pair(far, 4, 1, F)
    right = lax.dot_general(
        cols[width : width + EXTRA, :], cols[0:width, :], by_lane, preferred_element_type=jnp.float32
    )
    right_ref[...] = right * (1.0 / math.sqrt(deep))
    group(3)
    group(5)
    lo_arrived(4)
    group(4)

    for copy in started:
        copy.wait_send()
    for owner, away in conditional:

        @pl.when(owner != row)
        def _():
            away.wait_send()


def on_device(design, observations, filter_taps, tap_count, arc_id):
    here, width = design.shape
    deep = here * ROWS
    part = width // NZ
    vmem = pl.BlockSpec(memory_space=pltpu.VMEM)
    dma = pltpu.SemaphoreType.DMA
    bf16 = jnp.bfloat16
    normal, right = pl.pallas_call(
        body,
        out_shape=(
            jax.ShapeDtypeStruct((4, NZ, part, width), jnp.float32),
            jax.ShapeDtypeStruct((EXTRA, width), jnp.float32),
        ),
        in_specs=[vmem, vmem, vmem, pl.BlockSpec(memory_space=pltpu.SMEM), vmem],
        out_specs=(vmem, vmem),
        scratch_shapes=[
            pltpu.VMEM((width + EXTRA, deep), bf16),
            pltpu.VMEM((NZ, 4, part, deep), bf16),
            pltpu.VMEM((NZ, part, here), bf16),
            pltpu.VMEM((128, width), bf16),
            pltpu.VMEM((EXTRA, here), bf16),
            pltpu.VMEM((EXTRA, here), bf16),
            pltpu.VMEM((8, here), jnp.float32),
            dma((2,)), dma((2,)), dma((NZ,)), dma((NZ,)), dma((1,)), dma((NZ,)), dma((ROWS,)),
            dma((7,)), dma((7,)), dma((2, 5, 3)), dma((2, 5, 3)), dma((9,)), dma((9,)),
            dma((NZ, 2, 2)), dma((NZ, 2, 2)),
        ],
        compiler_params=pltpu.CompilerParams(
            collective_id=0, has_side_effects=True, vmem_limit_bytes=44 * 1024 * 1024
        ),
    )(
        design,
        observations.reshape(1, here),
        filter_taps.reshape(1, -1),
        tap_count,
        arc_id.reshape(ROWS, here),
    )
    return normal.reshape(4 * width, width), right[0]


def solution(mesh):
    finer = Mesh(mesh.devices.reshape(4, 2, 8, 2, 2), AXES)
    row, col = ("x", "yh"), ("z", "yl", "core")
    in_specs = (P(row, col), P(row), P(), P(), P())
    out_specs = (P(row, col), P(col))
    return jax.shard_map(
        on_device, mesh=finer, in_specs=in_specs, out_specs=out_specs, check_vma=False
    )
```

```python
import functools
import math

import jax
import jax.numpy as jnp
from jax import lax
from jax.experimental import pallas as pl
from jax.experimental.pallas import tpu as pltpu
from jax.sharding import Mesh
from jax.sharding import PartitionSpec as P

MESH = pl.DeviceIdType.MESH
AXES = ("x", "yh", "z", "yl", "core")
NX, NZ = 4, 8
ROWS = 8
EXTRA = 16
UP, DOWN = 0, 1


def body(
    taps, arcs, design_ref, table_ref,
    out_ref, right_ref,
    cols, panel, parts, halo, halo_obs, obs_own, table,
    halo_send, halo_recv, part_send, part_recv, panel_send, panel_recv,
    col_send, col_recv, z_send, z_recv, lo_send, lo_recv, pair_send, pair_recv,
):
    x, yh, z = lax.axis_index("x"), lax.axis_index("yh"), lax.axis_index("z")
    yl, core = lax.axis_index("yl"), lax.axis_index("core")
    row = x * 2 + yh
    mine = yl * 2 + core
    here, width = design_ref.shape
    part = width // NZ
    deep = here * ROWS
    half = deep // 2

    def at_row(r):
        return {"x": r // 2, "yh": lax.rem(r, 2)}

    barrier = pltpu.get_barrier_semaphore()
    peers = [at_row(lax.rem(row + i, ROWS)) for i in range(1, ROWS)]
    peers += [{"z": lax.rem(z + i, NZ)} for i in range(1, NZ)]
    peers += [{"yl": 1 - yl}, {"core": 1 - core}]
    for peer in peers:
        pl.semaphore_signal(barrier, inc=1, device_id=peer, device_id_type=MESH)

    table[...] = table_ref[...].reshape(table.shape)
    obs_own[...] = jnp.broadcast_to(table[ROWS : ROWS + 1, :], obs_own.shape).astype(jnp.bfloat16)
    halo[0:taps, :] = jnp.zeros((taps, width), jnp.bfloat16)

    started = []

    def send(src, dst, send_sem, recv_sem, device):
        copy = pltpu.make_async_remote_copy(
            src_ref=src, dst_ref=dst, send_sem=send_sem, recv_sem=recv_sem,
            device_id=device, device_id_type=MESH,
        )
        copy.start()
        started.append(copy)

    def arrived(dst, sem):
        pltpu.make_async_copy(dst, dst, sem).wait()

    line = jnp.broadcast_to(table[ROWS + 1 : ROWS + 2, :], (here, here))
    toeplitz = pltpu.roll(line, 0, 1, stride=1, stride_axis=0).T
    target = lax.broadcasted_iota(jnp.int32, (here, here), 0)
    source = lax.broadcasted_iota(jnp.int32, (here, here), 1)
    lag = target - source
    own = lag >= 0
    lag = jnp.where(own, lag, lag + here)
    arc_here = jnp.broadcast_to(table[pl.ds(row, 1), :], (here, here))
    arc_before = jnp.broadcast_to(table[pl.ds(jnp.maximum(row - 1, 0), 1), :], (here, here))
    arc_before = jnp.where(row > 0, arc_before, -1.0)
    arc_target = arc_here.T
    arc_source = jnp.where(own, arc_here, arc_before)
    limit = jnp.zeros((here, here), jnp.float32)
    for a in range(arcs):
        count = jnp.broadcast_to(table[ROWS + 2 : ROWS + 3, a : a + 1], (here, here))
        limit = jnp.where(arc_target == a, count, limit)
    rows_f = jnp.where(
        (arc_target == arc_source) & (lag.astype(jnp.float32) < limit) & (lag < taps), toeplitz, 0.0
    )

    def three(value):
        high = value.astype(jnp.bfloat16)
        rest = value - high.astype(jnp.float32)
        middle = rest.astype(jnp.bfloat16)
        return high, middle, (rest - middle.astype(jnp.float32)).astype(jnp.bfloat16)

    mid = here // 2
    by_lane = (((1,), (1,)), ((), ()))

    def total(terms, value):
        return sum(jnp.dot(t, value, preferred_element_type=jnp.float32) for t in terms[::-1])

    def total_lanes(terms, value):
        return sum(
            lax.dot_general(value, t, by_lane, preferred_element_type=jnp.float32) for t in terms[::-1]
        )

    F, H = 0, 1

    def lanes_of(r, h):
        return pl.ds(pl.multiple_of(h * half + r * mid, mid), mid)

    late = three(rows_f[mid:, :])
    cols[0:width, lanes_of(row, F)] = total(late, design_ref[...]).T.astype(jnp.bfloat16)
    cols[width : width + EXTRA, lanes_of(row, F)] = total_lanes(late, obs_own[...]).astype(jnp.bfloat16)
    early = three(jnp.where(own, rows_f, 0.0)[0:mid, 0:mid])
    before = three(jnp.where(own, 0.0, rows_f)[0:mid, here - 2 * taps :])

    def shard(r, h):
        return cols.at[:, lanes_of(r, h)]

    def own_part(q, h):
        return cols.at[pl.ds(pl.multiple_of(q * part, part), part), lanes_of(row, h)]

    right_x, left_x = lax.rem(x + 1, NX), lax.rem(x + NX - 1, NX)
    far_x = lax.rem(x + 2, NX)
    partner = x * 2 + 1 - yh
    near_first = [1, 7, 2, 6, 3, 5, 4]

    def pass_parts(h):
        for i in near_first:
            q = lax.rem(z + i, NZ)
            send(own_part(q, h), parts.at[h, z], part_send.at[h, i], part_recv.at[h, i], {"z": q})

    def pass_col(r, h, slot, device):
        send(shard(r, h), shard(r, h), col_send.at[h, slot], col_recv.at[h, slot], device)

    def col_arrived(r, h, slot):
        arrived(shard(r, h), col_recv.at[h, slot])

    def col_own(h):
        pass_col(row, h, 0, {"yh": 1 - yh})
        pass_col(row, h, 1, {"x": right_x})
        pass_col(row, h, 2, {"x": left_x})

    def col_first(h):
        col_arrived(partner, h, 0)
        pass_col(partner, h, 3, {"x": right_x})
        pass_col(partner, h, 4, {"x": left_x})
        col_arrived(left_x * 2 + yh, h, 1)
        pass_col(left_x * 2 + yh, h, 5, {"x": right_x})

    def col_second(h):
        col_arrived(right_x * 2 + 1 - yh, h, 4)
        pass_col(right_x * 2 + 1 - yh, h, 6, {"x": left_x})

    def col_last(h):
        col_arrived(left_x * 2 + 1 - yh, h, 3)
        col_arrived(right_x * 2 + yh, h, 2)
        col_arrived(far_x * 2 + yh, h, 5)
        col_arrived(far_x * 2 + 1 - yh, h, 6)

    conditional = []

    def pass_rows(h):
        for i in [0] + near_first:
            owner = lax.rem(z + NZ - i, NZ)
            source = parts.at[h, owner]
            if i == 0:
                source = own_part(z, h)
            else:
                arrived(source, part_recv.at[h, i])
            target_ref = panel.at[z, mine, :, lanes_of(row, h)]
            away = pltpu.make_async_remote_copy(
                src_ref=source, dst_ref=target_ref, send_sem=panel_send.at[h, i],
                recv_sem=panel_recv.at[h, row], device_id=at_row(owner), device_id_type=MESH,
            )
            local = pltpu.make_async_copy(source, target_ref, panel_recv.at[h, row])

            @pl.when(owner != row)
            def _():
                away.start()

            @pl.when(owner == row)
            def _():
                local.start()

            conditional.append((owner, away))

    above, below = {"z": lax.rem(z + 1, NZ)}, {"z": lax.rem(z + NZ - 1, NZ)}
    z_device = (above, below)

    def piece(q, other, h, other_core=False):
        line_of = 1 - yl if other else yl
        core_of = 1 - core if other_core else core
        return panel.at[q, line_of * 2 + core_of, :, h * half : (h + 1) * half]

    def halves(q, side):
        return panel.at[q, mine, side * (part // 2) : (side + 1) * (part // 2), half:deep]

    def pass_z(ref, way, d, kind):
        send(ref, ref, z_send.at[way, d, kind], z_recv.at[way, d, kind], z_device[way])

    def pass_lo(ref, slot):
        send(ref, ref, lo_send.at[slot], lo_recv.at[slot], {"yl": 1 - yl})

    def pass_pair(q, o, other, h):
        ref = piece(q, other, h)
        send(ref, ref, pair_send.at[o, other, h], pair_recv.at[o, other, h], {"core": 1 - core})

    def panel_arrived(h):
        for e in range(ROWS):
            start = h * half + e * mid
            arrived(panel.at[z, mine, :, start : start + mid], panel_recv.at[h, e])

    def group(o):
        q = lax.rem(z + NZ - o, NZ)
        for other in (0, 1):
            for h in (F, H):
                arrived(piece(q, other, h, True), pair_recv.at[o, other, h])
        tile = width // 3

        @pl.loop(0, 3)
        def _(n):
            lanes = pl.ds(pl.multiple_of(n * tile, tile), tile)
            result = lax.dot_general(
                panel[q].reshape(4 * part, deep), cols[lanes, :], by_lane,
                preferred_element_type=jnp.float32,
            )
            out_ref[:, q, :, lanes] = result.reshape(4, part, tile) * (1.0 / deep)

    def lo_arrived(o):
        q = lax.rem(z + NZ - o, NZ)
        arrived(piece(q, 1, H), lo_recv.at[o])
        pass_pair(q, o, 1, H)

    kinds = ((0, F), (0, H), (1, F))

    def hop(d, kind):
        other, h = kinds[kind]
        for way in (UP, DOWN):
            o = d if way == UP else NZ - d
            q = lax.rem(z + NZ - o, NZ)
            ref = piece(q, other, h)
            arrived(ref, z_recv.at[way, d, kind])
            if d < 3:
                pass_z(ref, way, d + 1, kind)
            elif kind == 1:
                pass_z(halves(q, way), way, d + 1, kind)
            elif kind == (0 if way == UP else 2):
                pass_z(ref, way, d + 1, kind)
            if kind == 1:
                pass_lo(ref, o)
            pass_pair(q, o, other, h)

    pl.semaphore_wait(barrier, len(peers))
    after = at_row(lax.rem(row + 1, ROWS))
    send(design_ref.at[here - taps : here, :], halo.at[taps : 2 * taps, :], halo_send.at[0], halo_recv.at[0], after)
    send(obs_own, halo_obs, halo_send.at[1], halo_recv.at[1], after)
    pass_parts(F)
    col_own(F)

    arrived(halo.at[taps : 2 * taps, :], halo_recv.at[0])
    arrived(halo_obs, halo_recv.at[1])
    white = total(early, design_ref[0:mid, :]) + total(before, halo[...])
    cols[0:width, lanes_of(row, H)] = white.T.astype(jnp.bfloat16)
    obs_white = total_lanes(early, obs_own[:, 0:mid]) + total_lanes(before, halo_obs[:, here - 2 * taps :])
    cols[width : width + EXTRA, lanes_of(row, H)] = obs_white.astype(jnp.bfloat16)
    pass_parts(H)
    pass_rows(F)
    pass_rows(H)
    col_own(H)
    panel_arrived(F)
    own_f = piece(z, 0, F)
    pass_lo(own_f, NZ)
    pass_z(own_f, UP, 1, 0)
    pass_z(own_f, DOWN, 1, 0)
    pass_pair(z, 0, 0, F)
    panel_arrived(H)
    own_h = piece(z, 0, H)
    pass_z(own_h, UP, 1, 1)
    pass_z(own_h, DOWN, 1, 1)
    pass_lo(own_h, 0)
    pass_pair(z, 0, 0, H)

    other_f = piece(z, 1, F)
    arrived(other_f, lo_recv.at[NZ])
    pass_z(other_f, UP, 1, 2)
    pass_z(other_f, DOWN, 1, 2)
    pass_pair(z, 0, 1, F)
    col_first(F)

    hop(1, 0)
    col_first(H)
    hop(1, 1)
    col_second(F)
    lo_arrived(0)
    hop(1, 2)
    col_second(H)
    hop(2, 0)
    lo_arrived(1)
    hop(2, 1)
    lo_arrived(7)
    hop(2, 2)
    col_last(F)
    col_last(H)
    group(0)
    group(1)
    hop(3, 1)
    group(7)
    hop(3, 0)
    lo_arrived(2)
    group(2)
    hop(3, 2)
    lo_arrived(6)
    group(6)
    far = lax.rem(z + 4, NZ)
    for way in (UP, DOWN):
        arrived(halves(far, way), z_recv.at[way, 4, 1])
    pass_lo(piece(far, 0, H), 4)
    pass_pair(far, 4, 0, H)
    lo_arrived(3)
    lo_arrived(5)
    right = lax.dot_general(
        cols[width : width + EXTRA, :], cols[0:width, :], by_lane, preferred_element_type=jnp.float32
    )
    right_ref[...] = right * (1.0 / math.sqrt(deep))
    group(3)
    arrived(piece(far, 0, F), z_recv.at[UP, 4, 0])
    pass_pair(far, 4, 0, F)
    arrived(piece(far, 1, F), z_recv.at[DOWN, 4, 2])
    pass_pair(far, 4, 1, F)
    group(5)
    lo_arrived(4)
    group(4)

    for copy in started:
        copy.wait_send()
    for owner, away in conditional:

        @pl.when(owner != row)
        def _():
            away.wait_send()


def on_device(design, observations, filter_taps, tap_count, arc_id):
    here, width = design.shape
    taps, arcs = filter_taps.shape[0], tap_count.shape[0]
    deep = here * ROWS
    part = width // NZ
    vmem = pl.BlockSpec(memory_space=pltpu.VMEM)
    dma = pltpu.SemaphoreType.DMA
    bf16, f32 = jnp.bfloat16, jnp.float32
    table = jnp.concatenate(
        [
            arc_id.astype(f32),
            observations.astype(f32),
            jnp.pad(filter_taps, (0, here - taps)),
            jnp.pad(tap_count.astype(f32), (0, 6 * here - arcs)),
        ]
    )
    normal, right = pl.pallas_call(
        functools.partial(body, taps, arcs),
        out_shape=(
            jax.ShapeDtypeStruct((4, NZ, part, width), f32),
            jax.ShapeDtypeStruct((EXTRA, width), f32),
        ),
        in_specs=[vmem, vmem],
        out_specs=(vmem, vmem),
        scratch_shapes=[
            pltpu.VMEM((width + EXTRA, deep), bf16),
            pltpu.VMEM((NZ, 4, part, deep), bf16),
            pltpu.VMEM((2, NZ, part, here // 2), bf16),
            pltpu.VMEM((2 * taps, width), bf16),
            pltpu.VMEM((EXTRA, here), bf16),
            pltpu.VMEM((EXTRA, here), bf16),
            pltpu.VMEM((16, here), f32),
            dma((2,)), dma((2,)), dma((2, NZ)), dma((2, NZ)), dma((2, NZ)), dma((2, ROWS)),
            dma((2, 7)), dma((2, 7)), dma((2, 5, 3)), dma((2, 5, 3)), dma((9,)), dma((9,)),
            dma((NZ, 2, 2)), dma((NZ, 2, 2)),
        ],
        compiler_params=pltpu.CompilerParams(
            collective_id=0, has_side_effects=True, vmem_limit_bytes=44 * 1024 * 1024
        ),
    )(design, table)
    return normal.reshape(4 * width, width), right[0]


def solution(mesh):
    finer = Mesh(mesh.devices.reshape(4, 2, 8, 2, 2), AXES)
    row, col = ("x", "yh"), ("z", "yl", "core")
    in_specs = (P(row, col), P(row), P(), P(), P())
    out_specs = (P(row, col), P(col))
    return jax.shard_map(
        on_device, mesh=finer, in_specs=in_specs, out_specs=out_specs, check_vma=False
    )
```

```python
import functools
import math

import jax
import jax.numpy as jnp
from jax import lax
from jax.experimental import pallas as pl
from jax.experimental.pallas import tpu as pltpu
from jax.sharding import Mesh
from jax.sharding import PartitionSpec as P

MESH = pl.DeviceIdType.MESH
LIMIT1, LIMIT2 = 28, 28
AXES = ("x", "yh", "z", "yl", "core")
NX, NZ = 4, 8
ROWS = 8
EXTRA = 16
UP, DOWN = 0, 1

LATER = (5, 4)
EARLY = 80
LATE_SIDES = (0,)
BY_LANE = (((1,), (1,)), ((), ()))


def multiply(panel, cols, out_ref, q, slot):
    _, lines, part, deep = panel.shape
    width = out_ref.shape[-1]
    tile = width // 3

    @pl.loop(0, 3)
    def _(n):
        lanes = pl.ds(pl.multiple_of(n * tile, tile), tile)
        result = lax.dot_general(
            panel[q].reshape(lines * part, deep), cols[lanes, :], BY_LANE, preferred_element_type=jnp.float32
        )
        out_ref[:, slot, :, lanes] = result.reshape(lines, part, tile) * (1.0 / deep)


def finish(done, cols, panel, out_ref, right_ref, last, sems):
    width = done.shape[-1]
    deep = panel.shape[-1]
    z = lax.axis_index("z")
    copies = []

    def write(source, q):
        copy = pltpu.make_async_copy(source, out_ref.at[:, q], sems.at[len(copies)])
        copy.start()
        copies.append(copy)

    for o in range(NZ):
        q = lax.rem(z + NZ - o, NZ)
        if o not in LATER:
            write(done.at[:, q], q)
    for slot, o in enumerate(LATER):
        q = lax.rem(z + NZ - o, NZ)
        multiply(panel, cols, last, q, slot)
        write(last.at[:, slot], q)
    right = lax.dot_general(cols[width:, :], cols[0:width, :], BY_LANE, preferred_element_type=jnp.float32)
    right_ref[...] = right[0:1, :].reshape(width) * (1.0 / math.sqrt(deep))
    for copy in copies:
        copy.wait()


def body(
    taps, arcs, design_ref, table_ref,
    out_ref, cols, panel,
    parts, halo, halo_obs, obs_own, table,
    halo_send, halo_recv, part_send, part_recv, panel_send, panel_recv,
    col_send, col_recv, z_send, z_recv, lo_send, lo_recv, pair_send, pair_recv,
):
    x, yh, z = lax.axis_index("x"), lax.axis_index("yh"), lax.axis_index("z")
    yl, core = lax.axis_index("yl"), lax.axis_index("core")
    row = x * 2 + yh
    mine = yl * 2 + core
    here, width = design_ref.shape
    part = width // NZ
    deep = here * ROWS
    half = deep // 2

    def at_row(r):
        return {"x": r // 2, "yh": lax.rem(r, 2)}

    barrier = pltpu.get_barrier_semaphore()
    peers = [at_row(lax.rem(row + i, ROWS)) for i in range(1, ROWS)]
    peers += [{"z": lax.rem(z + i, NZ)} for i in range(1, NZ)]
    peers += [{"yl": 1 - yl}, {"core": 1 - core}]
    for peer in peers:
        pl.semaphore_signal(barrier, inc=1, device_id=peer, device_id_type=MESH)

    table[...] = table_ref[...].reshape(table.shape)
    obs_own[...] = jnp.broadcast_to(table[ROWS : ROWS + 1, :], obs_own.shape).astype(jnp.bfloat16)
    halo[0:taps, :] = jnp.zeros((taps, width), jnp.bfloat16)

    started = []

    def send(src, dst, send_sem, recv_sem, device):
        copy = pltpu.make_async_remote_copy(
            src_ref=src, dst_ref=dst, send_sem=send_sem, recv_sem=recv_sem,
            device_id=device, device_id_type=MESH,
        )
        copy.start()
        started.append(copy)

    def arrived(dst, sem):
        pltpu.make_async_copy(dst, dst, sem).wait()

    line = jnp.broadcast_to(table[ROWS + 1 : ROWS + 2, :], (here, here))
    toeplitz = pltpu.roll(line, 0, 1, stride=1, stride_axis=0).T
    target = lax.broadcasted_iota(jnp.int32, (here, here), 0)
    source = lax.broadcasted_iota(jnp.int32, (here, here), 1)
    lag = target - source
    own = lag >= 0
    lag = jnp.where(own, lag, lag + here)
    arc_here = jnp.broadcast_to(table[pl.ds(row, 1), :], (here, here))
    arc_before = jnp.broadcast_to(table[pl.ds(jnp.maximum(row - 1, 0), 1), :], (here, here))
    arc_before = jnp.where(row > 0, arc_before, -1.0)
    arc_target = arc_here.T
    arc_source = jnp.where(own, arc_here, arc_before)
    limit = jnp.zeros((here, here), jnp.float32)
    for a in range(arcs):
        count = jnp.broadcast_to(table[ROWS + 2 : ROWS + 3, a : a + 1], (here, here))
        limit = jnp.where(arc_target == a, count, limit)
    rows_f = jnp.where(
        (arc_target == arc_source) & (lag.astype(jnp.float32) < limit) & (lag < taps), toeplitz, 0.0
    )

    def three(value):
        high = value.astype(jnp.bfloat16)
        rest = value - high.astype(jnp.float32)
        middle = rest.astype(jnp.bfloat16)
        return high, middle, (rest - middle.astype(jnp.float32)).astype(jnp.bfloat16)

    mid = here // 2
    by_lane = (((1,), (1,)), ((), ()))

    def total(terms, value):
        return sum(jnp.dot(t, value, preferred_element_type=jnp.float32) for t in terms[::-1])

    def total_lanes(terms, value):
        return sum(
            lax.dot_general(value, t, by_lane, preferred_element_type=jnp.float32) for t in terms[::-1]
        )

    H, F = 0, 1

    def lanes_of(r, h):
        return pl.ds(pl.multiple_of(h * half + r * mid, mid), mid)

    late = three(rows_f[mid:, :])
    cols[0:width, lanes_of(row, H)] = total(late, design_ref[...]).T.astype(jnp.bfloat16)
    cols[width : width + EXTRA, lanes_of(row, H)] = total_lanes(late, obs_own[...]).astype(jnp.bfloat16)
    early = three(jnp.where(own, rows_f, 0.0)[0:mid, 0:mid])
    before = three(jnp.where(own, 0.0, rows_f)[0:mid, here - 2 * taps :])

    def shard(r, h):
        return cols.at[:, lanes_of(r, h)]

    def own_part(q, h):
        return cols.at[pl.ds(pl.multiple_of(q * part, part), part), lanes_of(row, h)]

    right_x, left_x = lax.rem(x + 1, NX), lax.rem(x + NX - 1, NX)
    far_x = lax.rem(x + 2, NX)
    partner = x * 2 + 1 - yh
    near_first = [1, 7, 2, 6, 3, 5, 4]

    def pass_parts(h):
        for i in near_first:
            q = lax.rem(z + i, NZ)
            send(own_part(q, h), parts.at[h, z], part_send.at[h, i], part_recv.at[h, i], {"z": q})

    def pass_col(r, h, slot, device):
        send(shard(r, h), shard(r, h), col_send.at[h, slot], col_recv.at[h, slot], device)

    def col_arrived(r, h, slot):
        arrived(shard(r, h), col_recv.at[h, slot])

    def col_y(h):
        pass_col(row, h, 0, {"yh": 1 - yh})

    def col_x(h):
        pass_col(row, h, 1, {"x": right_x})
        pass_col(row, h, 2, {"x": left_x})

    def col_first(h):
        col_arrived(partner, h, 0)
        pass_col(partner, h, 3, {"x": right_x})
        pass_col(partner, h, 4, {"x": left_x})
        col_arrived(left_x * 2 + yh, h, 1)
        pass_col(left_x * 2 + yh, h, 5, {"x": right_x})

    def col_second(h):
        col_arrived(right_x * 2 + 1 - yh, h, 4)
        pass_col(right_x * 2 + 1 - yh, h, 6, {"x": left_x})

    def col_last(h):
        col_arrived(left_x * 2 + 1 - yh, h, 3)
        col_arrived(right_x * 2 + yh, h, 2)
        col_arrived(far_x * 2 + yh, h, 5)
        col_arrived(far_x * 2 + 1 - yh, h, 6)

    conditional = []

    def pass_rows(h):
        for i in [0] + near_first:
            owner = lax.rem(z + NZ - i, NZ)
            source = parts.at[h, owner]
            if i == 0:
                source = own_part(z, h)
            else:
                arrived(source, part_recv.at[h, i])
            target_ref = panel.at[z, mine, :, lanes_of(row, h)]
            away = pltpu.make_async_remote_copy(
                src_ref=source, dst_ref=target_ref, send_sem=panel_send.at[h, i],
                recv_sem=panel_recv.at[h, row], device_id=at_row(owner), device_id_type=MESH,
            )
            local = pltpu.make_async_copy(source, target_ref, panel_recv.at[h, row])

            @pl.when(owner != row)
            def _():
                away.start()

            @pl.when(owner == row)
            def _():
                local.start()

            conditional.append((owner, away))

    above, below = {"z": lax.rem(z + 1, NZ)}, {"z": lax.rem(z + NZ - 1, NZ)}
    z_device = (above, below)

    def piece(q, other, h, other_core=False):
        line_of = 1 - yl if other else yl
        core_of = 1 - core if other_core else core
        return panel.at[q, line_of * 2 + core_of, :, h * half : (h + 1) * half]

    def halves(q, side):
        return panel.at[q, mine, side * (part // 2) : (side + 1) * (part // 2), 0:half]

    def early_rows(q, other):
        line_of = 1 - yl if other else yl
        return panel.at[q, line_of * 2 + core, 0:EARLY, half:deep]

    def late_rows(q, other):
        line_of = 1 - yl if other else yl
        return panel.at[q, line_of * 2 + core, EARLY:part, half:deep]

    def late_side(q, side):
        cut = EARLY + (part - EARLY) // 2 if len(LATE_SIDES) == 2 else part
        start, stop = (EARLY, cut) if side == UP else (cut, part)
        return panel.at[q, mine, start:stop, half:deep]

    def pass_z(ref, way, d, kind):
        send(ref, ref, z_send.at[way, d, kind], z_recv.at[way, d, kind], z_device[way])

    def pass_lo(ref, slot):
        send(ref, ref, lo_send.at[slot], lo_recv.at[slot], {"yl": 1 - yl})

    def pass_pair(q, o, other, h):
        ref = piece(q, other, h)
        send(ref, ref, pair_send.at[o, other, h], pair_recv.at[o, other, h], {"core": 1 - core})

    def panel_arrived(h):
        for e in range(ROWS):
            start = h * half + e * mid
            arrived(panel.at[z, mine, :, start : start + mid], panel_recv.at[h, e])

    def group(o):
        q = lax.rem(z + NZ - o, NZ)
        for other in (0, 1):
            for h in (F, H):
                arrived(piece(q, other, h, True), pair_recv.at[o, other, h])
        if o not in LATER:
            multiply(panel, cols, out_ref, q, q)

    def lo_arrived(o):
        q = lax.rem(z + NZ - o, NZ)
        arrived(piece(q, 1, H), lo_recv.at[o])
        pass_pair(q, o, 1, H)
        arrived(late_rows(q, 1), lo_recv.at[NZ + 1 + o])
        pass_pair(q, o, 1, F)

    EARLY_OWN, LATE, HALF, EARLY_OTHER = 0, 1, 2, 3

    def ref_of(q, kind):
        if kind == EARLY_OWN:
            return early_rows(q, 0)
        if kind == LATE:
            return late_rows(q, 0)
        if kind == HALF:
            return piece(q, 0, H)
        return early_rows(q, 1)

    def onward(q, o, kind):
        if kind == LATE:
            pass_lo(late_rows(q, 0), NZ + 1 + o)
        elif kind == HALF:
            pass_lo(piece(q, 0, H), o)
            pass_pair(q, o, 0, H)
        elif kind == EARLY_OWN:
            pass_pair(q, o, 0, F)

    def hop(d, kind):
        for way in (UP, DOWN):
            o = d if way == UP else NZ - d
            q = lax.rem(z + NZ - o, NZ)
            ref = ref_of(q, kind)
            arrived(ref, z_recv.at[way, d, kind])
            if d < 3:
                pass_z(ref, way, d + 1, kind)
            elif kind == HALF:
                pass_z(halves(q, way), way, d + 1, kind)
            elif kind == LATE and way in LATE_SIDES:
                pass_z(late_side(q, way), way, d + 1, kind)
            elif kind == (EARLY_OWN if way == UP else EARLY_OTHER):
                pass_z(ref, way, d + 1, kind)
            onward(q, o, kind)

    pl.semaphore_wait(barrier, len(peers))
    after = at_row(lax.rem(row + 1, ROWS))
    send(design_ref.at[here - taps : here, :], halo.at[taps : 2 * taps, :], halo_send.at[0], halo_recv.at[0], after)
    send(obs_own, halo_obs, halo_send.at[1], halo_recv.at[1], after)
    pass_parts(H)
    col_y(H)
    col_x(H)

    arrived(halo.at[taps : 2 * taps, :], halo_recv.at[0])
    arrived(halo_obs, halo_recv.at[1])
    white = total(early, design_ref[0:mid, :]) + total(before, halo[...])
    cols[0:width, lanes_of(row, F)] = white.T.astype(jnp.bfloat16)
    obs_white = total_lanes(early, obs_own[:, 0:mid]) + total_lanes(before, halo_obs[:, here - 2 * taps :])
    cols[width : width + EXTRA, lanes_of(row, F)] = obs_white.astype(jnp.bfloat16)
    pass_parts(F)
    pass_rows(H)
    pass_rows(F)
    col_x(F)
    panel_arrived(H)
    pass_lo(piece(z, 0, H), 0)
    pass_z(ref_of(z, HALF), UP, 1, HALF)
    pass_z(ref_of(z, HALF), DOWN, 1, HALF)
    pass_pair(z, 0, 0, H)
    panel_arrived(F)
    pass_lo(early_rows(z, 0), NZ)
    for kind in (LATE, EARLY_OWN):
        pass_z(ref_of(z, kind), UP, 1, kind)
        pass_z(ref_of(z, kind), DOWN, 1, kind)
        onward(z, 0, kind)
    col_y(F)
    col_first(H)
    arrived(early_rows(z, 1), lo_recv.at[NZ])
    pass_z(early_rows(z, 1), UP, 1, EARLY_OTHER)
    pass_z(early_rows(z, 1), DOWN, 1, EARLY_OTHER)

    hop(1, HALF)
    hop(1, LATE)
    hop(1, EARLY_OWN)
    col_second(H)
    hop(1, EARLY_OTHER)
    col_first(F)
    lo_arrived(0)
    hop(2, HALF)
    lo_arrived(1)
    hop(2, LATE)
    hop(2, EARLY_OWN)
    lo_arrived(7)
    col_second(F)
    hop(2, EARLY_OTHER)
    hop(3, HALF)
    col_last(H)
    col_last(F)
    group(0)
    hop(3, LATE)
    group(1)
    hop(3, EARLY_OWN)
    lo_arrived(2)
    group(7)
    hop(3, EARLY_OTHER)
    lo_arrived(6)
    group(2)
    far = lax.rem(z + 4, NZ)
    for way in (UP, DOWN):
        arrived(halves(far, way), z_recv.at[way, 4, HALF])
    onward(far, 4, HALF)
    for way in LATE_SIDES:
        arrived(late_side(far, way), z_recv.at[way, 4, LATE])
    onward(far, 4, LATE)
    group(6)
    lo_arrived(3)
    lo_arrived(5)
    group(3)
    arrived(early_rows(far, 0), z_recv.at[UP, 4, EARLY_OWN])
    onward(far, 4, EARLY_OWN)
    arrived(early_rows(far, 1), z_recv.at[DOWN, 4, EARLY_OTHER])
    group(5)
    lo_arrived(4)
    group(4)

    for copy in started:
        copy.wait_send()
    for owner, away in conditional:

        @pl.when(owner != row)
        def _():
            away.wait_send()


def on_device(design, observations, filter_taps, tap_count, arc_id):
    here, width = design.shape
    taps, arcs = filter_taps.shape[0], tap_count.shape[0]
    deep = here * ROWS
    part = width // NZ
    vmem = pl.BlockSpec(memory_space=pltpu.VMEM)
    dma = pltpu.SemaphoreType.DMA
    bf16, f32 = jnp.bfloat16, jnp.float32
    whole = 16 * here

    def spread(value, start):
        return jnp.pad(value, (start, whole - start - value.shape[0])).astype(f32)

    table = spread(arc_id, 0) + spread(observations, deep) + spread(filter_taps, deep + here) + spread(tap_count, deep + 2 * here)
    done, cols, panel = pl.pallas_call(
        functools.partial(body, taps, arcs),
        out_shape=(
            jax.ShapeDtypeStruct((4, NZ, part, width), f32),
            jax.ShapeDtypeStruct((width + EXTRA, deep), bf16),
            jax.ShapeDtypeStruct((NZ, 4, part, deep), bf16),
        ),
        in_specs=[vmem, vmem],
        out_specs=(vmem, vmem, vmem),
        scratch_shapes=[
            pltpu.VMEM((2, NZ, part, here // 2), bf16),
            pltpu.VMEM((2 * taps, width), bf16),
            pltpu.VMEM((EXTRA, here), bf16),
            pltpu.VMEM((EXTRA, here), bf16),
            pltpu.VMEM((16, here), f32),
            dma((2,)), dma((2,)), dma((2, NZ)), dma((2, NZ)), dma((2, NZ)), dma((2, ROWS)),
            dma((2, 7)), dma((2, 7)), dma((2, 5, 4)), dma((2, 5, 4)), dma((17,)), dma((17,)),
            dma((NZ, 2, 2)), dma((NZ, 2, 2)),
        ],
        compiler_params=pltpu.CompilerParams(
            collective_id=0, has_side_effects=True, vmem_limit_bytes=LIMIT1 * 1024 * 1024
        ),
    )(design, table)
    normal, right = pl.pallas_call(
        finish,
        out_shape=(
            jax.ShapeDtypeStruct((4, NZ, part, width), f32),
            jax.ShapeDtypeStruct((width,), f32),
        ),
        in_specs=[vmem, vmem, vmem],
        out_specs=(pl.BlockSpec(memory_space=pl.ANY), vmem),
        scratch_shapes=[pltpu.VMEM((4, len(LATER), part, width), f32), dma((NZ,))],
        compiler_params=pltpu.CompilerParams(vmem_limit_bytes=LIMIT2 * 1024 * 1024),
    )(done, cols, panel)
    return normal.reshape(4 * width, width), right


def solution(mesh):
    finer = Mesh(mesh.devices.reshape(4, 2, 8, 2, 2), AXES)
    row, col = ("x", "yh"), ("z", "yl", "core")
    in_specs = (P(row, col), P(row), P(), P(), P())
    out_specs = (P(row, col), P(col))
    return jax.shard_map(
        on_device, mesh=finer, in_specs=in_specs, out_specs=out_specs, check_vma=False
    )
```

```python
import functools
import math

import jax
import jax.numpy as jnp
from jax import lax
from jax.experimental import pallas as pl
from jax.experimental.pallas import tpu as pltpu
from jax.sharding import Mesh
from jax.sharding import PartitionSpec as P

MESH = pl.DeviceIdType.MESH
LIMIT1, LIMIT2 = 28, 28
AXES = ("x", "yh", "z", "yl", "core")
NX, NZ = 4, 8
ROWS = 8
EXTRA = 16
UP, DOWN = 0, 1

LATER = (4,)
EARLY = 80
LATE_SIDES = (0,)
BY_LANE = (((1,), (1,)), ((), ()))


def multiply(panel, cols, out_ref, q, slot):
    _, lines, part, deep = panel.shape
    width = out_ref.shape[-1]
    tile = width // 3

    @pl.loop(0, 3)
    def _(n):
        lanes = pl.ds(pl.multiple_of(n * tile, tile), tile)
        result = lax.dot_general(
            panel[q].reshape(lines * part, deep), cols[lanes, :], BY_LANE, preferred_element_type=jnp.float32
        )
        out_ref[:, slot, :, lanes] = result.reshape(lines, part, tile) * (1.0 / deep)


def finish(done, cols, panel, out_ref, right_ref, last, sems, tile_sems):
    width = done.shape[-1]
    deep = panel.shape[-1]
    z = lax.axis_index("z")
    copies = []

    def write(source, q):
        copy = pltpu.make_async_copy(source, out_ref.at[:, q], sems.at[len(copies)])
        copy.start()
        copies.append(copy)

    for o in range(NZ):
        q = lax.rem(z + NZ - o, NZ)
        if o not in LATER:
            write(done.at[:, q], q)
    tiles = 3
    tile = width // tiles

    def tile_copy(t):
        slot, n = t // tiles, lax.rem(t, tiles)
        q = lax.rem(z + NZ - LATER[0] + slot, NZ)
        lanes = pl.ds(pl.multiple_of(n * tile, tile), tile)
        return q, slot, lanes, pltpu.make_async_copy(
            last.at[:, slot, :, lanes], out_ref.at[:, q, :, lanes], tile_sems.at[t]
        )

    @pl.loop(0, tiles * len(LATER))
    def _(t):
        q, slot, lanes, copy = tile_copy(t)
        result = lax.dot_general(
            panel[q].reshape(-1, deep), cols[lanes, :], BY_LANE, preferred_element_type=jnp.float32
        )
        last[:, slot, :, lanes] = result.reshape(last.shape[0], -1, tile) * (1.0 / deep)
        copy.start()

    right = lax.dot_general(cols[width:, :], cols[0:width, :], BY_LANE, preferred_element_type=jnp.float32)
    right_ref[...] = right[0:1, :].reshape(width) * (1.0 / math.sqrt(deep))
    for copy in copies:
        copy.wait()

    @pl.loop(0, tiles * len(LATER))
    def _(t):
        tile_copy(t)[3].wait()


def body(
    taps, arcs, design_ref, table_ref,
    out_ref, cols, panel,
    parts, halo, halo_obs, obs_own, table,
    halo_send, halo_recv, part_send, part_recv, panel_send, panel_recv,
    col_send, col_recv, z_send, z_recv, lo_send, lo_recv, pair_send, pair_recv,
):
    x, yh, z = lax.axis_index("x"), lax.axis_index("yh"), lax.axis_index("z")
    yl, core = lax.axis_index("yl"), lax.axis_index("core")
    row = x * 2 + yh
    mine = yl * 2 + core
    here, width = design_ref.shape
    part = width // NZ
    deep = here * ROWS
    half = deep // 2

    def at_row(r):
        return {"x": r // 2, "yh": lax.rem(r, 2)}

    barrier = pltpu.get_barrier_semaphore()
    peers = [at_row(lax.rem(row + i, ROWS)) for i in range(1, ROWS)]
    peers += [{"z": lax.rem(z + i, NZ)} for i in range(1, NZ)]
    peers += [{"yl": 1 - yl}, {"core": 1 - core}]
    for peer in peers:
        pl.semaphore_signal(barrier, inc=1, device_id=peer, device_id_type=MESH)

    table[...] = table_ref[...].reshape(table.shape)
    obs_own[...] = jnp.broadcast_to(table[ROWS : ROWS + 1, :], obs_own.shape).astype(jnp.bfloat16)
    halo[0:taps, :] = jnp.zeros((taps, width), jnp.bfloat16)

    started = []

    def send(src, dst, send_sem, recv_sem, device):
        copy = pltpu.make_async_remote_copy(
            src_ref=src, dst_ref=dst, send_sem=send_sem, recv_sem=recv_sem,
            device_id=device, device_id_type=MESH,
        )
        copy.start()
        started.append(copy)

    def arrived(dst, sem):
        pltpu.make_async_copy(dst, dst, sem).wait()

    mid = here // 2
    line = jnp.broadcast_to(table[ROWS + 1 : ROWS + 2, :], (here, here))
    shifted = pltpu.roll(line, 0, 1, stride=1, stride_axis=0)
    arc_here = table[pl.ds(row, 1), :]
    arc_before = jnp.where(row > 0, table[pl.ds(jnp.maximum(row - 1, 0), 1), :], -1.0)
    counts = jnp.zeros((1, here), jnp.float32)
    for a in range(arcs):
        counts = jnp.where(arc_here == a, table[ROWS + 2 : ROWS + 3, a : a + 1], counts)

    def filter_rows(start):
        shape = (mid, here)
        lag = lax.broadcasted_iota(jnp.int32, shape, 0) + start - lax.broadcasted_iota(jnp.int32, shape, 1)
        own = lag >= 0
        lag = jnp.where(own, lag, lag + here)
        arc_target = jnp.broadcast_to(arc_here[:, start : start + mid], (mid, mid)).T
        limit = jnp.broadcast_to(counts[:, start : start + mid], (mid, mid)).T
        arc_target = jnp.concatenate([arc_target, arc_target], axis=1)
        limit = jnp.concatenate([limit, limit], axis=1)
        arc_source = jnp.where(own, arc_here, arc_before)
        used = (arc_target == arc_source) & (lag.astype(jnp.float32) < limit) & (lag < taps)
        return own, jnp.where(used, shifted[:, start : start + mid].T, 0.0)

    def three(value):
        high = value.astype(jnp.bfloat16)
        rest = value - high.astype(jnp.float32)
        middle = rest.astype(jnp.bfloat16)
        return high, middle, (rest - middle.astype(jnp.float32)).astype(jnp.bfloat16)

    by_lane = (((1,), (1,)), ((), ()))

    def total(terms, value):
        return sum(jnp.dot(t, value, preferred_element_type=jnp.float32) for t in terms[::-1])

    def total_lanes(terms, value):
        return sum(
            lax.dot_general(value, t, by_lane, preferred_element_type=jnp.float32) for t in terms[::-1]
        )

    H, F = 0, 1

    def lanes_of(r, h):
        return pl.ds(pl.multiple_of(h * half + r * mid, mid), mid)

    late = three(filter_rows(mid)[1])
    cols[0:width, lanes_of(row, H)] = total(late, design_ref[...]).T.astype(jnp.bfloat16)
    cols[width : width + EXTRA, lanes_of(row, H)] = total_lanes(late, obs_own[...]).astype(jnp.bfloat16)
    def shard(r, h):
        return cols.at[:, lanes_of(r, h)]

    def own_part(q, h):
        return cols.at[pl.ds(pl.multiple_of(q * part, part), part), lanes_of(row, h)]

    right_x, left_x = lax.rem(x + 1, NX), lax.rem(x + NX - 1, NX)
    far_x = lax.rem(x + 2, NX)
    partner = x * 2 + 1 - yh
    near_first = [1, 7, 2, 6, 3, 5, 4]

    def pass_parts(h):
        for i in near_first[::-1]:
            q = lax.rem(z + i, NZ)
            send(own_part(q, h), parts.at[h, z], part_send.at[h, i], part_recv.at[h, i], {"z": q})

    def pass_col(r, h, slot, device):
        send(shard(r, h), shard(r, h), col_send.at[h, slot], col_recv.at[h, slot], device)

    def col_arrived(r, h, slot):
        arrived(shard(r, h), col_recv.at[h, slot])

    def col_y(h):
        pass_col(row, h, 0, {"yh": 1 - yh})

    def col_x(h):
        pass_col(row, h, 1, {"x": right_x})
        pass_col(row, h, 2, {"x": left_x})

    def col_first(h):
        col_arrived(partner, h, 0)
        pass_col(partner, h, 3, {"x": right_x})
        pass_col(partner, h, 4, {"x": left_x})
        col_arrived(left_x * 2 + yh, h, 1)
        pass_col(left_x * 2 + yh, h, 5, {"x": right_x})

    def col_second(h):
        col_arrived(right_x * 2 + 1 - yh, h, 4)
        pass_col(right_x * 2 + 1 - yh, h, 6, {"x": left_x})

    def col_last(h):
        col_arrived(left_x * 2 + 1 - yh, h, 3)
        col_arrived(right_x * 2 + yh, h, 2)
        col_arrived(far_x * 2 + yh, h, 5)
        col_arrived(far_x * 2 + 1 - yh, h, 6)

    conditional = []

    def pass_rows(h):
        for i in [0] + near_first:
            owner = lax.rem(z + NZ - i, NZ)
            source = parts.at[h, owner]
            if i == 0:
                source = own_part(z, h)
            else:
                arrived(source, part_recv.at[h, i])
            target_ref = panel.at[z, mine, :, lanes_of(row, h)]
            away = pltpu.make_async_remote_copy(
                src_ref=source, dst_ref=target_ref, send_sem=panel_send.at[h, i],
                recv_sem=panel_recv.at[h, row], device_id=at_row(owner), device_id_type=MESH,
            )
            local = pltpu.make_async_copy(source, target_ref, panel_recv.at[h, row])

            @pl.when(owner != row)
            def _():
                away.start()

            @pl.when(owner == row)
            def _():
                local.start()

            conditional.append((owner, away))

    above, below = {"z": lax.rem(z + 1, NZ)}, {"z": lax.rem(z + NZ - 1, NZ)}
    z_device = (above, below)

    def piece(q, other, h, other_core=False):
        line_of = 1 - yl if other else yl
        core_of = 1 - core if other_core else core
        return panel.at[q, line_of * 2 + core_of, :, h * half : (h + 1) * half]

    def halves(q, side):
        return panel.at[q, mine, side * (part // 2) : (side + 1) * (part // 2), 0:half]

    def early_rows(q, other):
        line_of = 1 - yl if other else yl
        return panel.at[q, line_of * 2 + core, 0:EARLY, half:deep]

    def late_rows(q, other):
        line_of = 1 - yl if other else yl
        return panel.at[q, line_of * 2 + core, EARLY:part, half:deep]

    def late_side(q, side):
        cut = EARLY + (part - EARLY) // 2 if len(LATE_SIDES) == 2 else part
        start, stop = (EARLY, cut) if side == UP else (cut, part)
        return panel.at[q, mine, start:stop, half:deep]

    def pass_z(ref, way, d, kind):
        send(ref, ref, z_send.at[way, d, kind], z_recv.at[way, d, kind], z_device[way])

    def pass_lo(ref, slot):
        send(ref, ref, lo_send.at[slot], lo_recv.at[slot], {"yl": 1 - yl})

    def pass_pair(q, o, other, h):
        ref = piece(q, other, h)
        send(ref, ref, pair_send.at[o, other, h], pair_recv.at[o, other, h], {"core": 1 - core})

    def panel_arrived(h):
        for e in range(ROWS):
            start = h * half + e * mid
            arrived(panel.at[z, mine, :, start : start + mid], panel_recv.at[h, e])

    def group(o):
        q = lax.rem(z + NZ - o, NZ)
        for other in (0, 1):
            for h in (F, H):
                arrived(piece(q, other, h, True), pair_recv.at[o, other, h])
        if o not in LATER:
            multiply(panel, cols, out_ref, q, q)

    def lo_arrived(o):
        q = lax.rem(z + NZ - o, NZ)
        arrived(piece(q, 1, H), lo_recv.at[o])
        pass_pair(q, o, 1, H)
        arrived(late_rows(q, 1), lo_recv.at[NZ + 1 + o])
        pass_pair(q, o, 1, F)

    EARLY_OWN, LATE, HALF, EARLY_OTHER = 0, 1, 2, 3

    def ref_of(q, kind):
        if kind == EARLY_OWN:
            return early_rows(q, 0)
        if kind == LATE:
            return late_rows(q, 0)
        if kind == HALF:
            return piece(q, 0, H)
        return early_rows(q, 1)

    def onward(q, o, kind):
        if kind == LATE:
            pass_lo(late_rows(q, 0), NZ + 1 + o)
        elif kind == HALF:
            pass_lo(piece(q, 0, H), o)
            pass_pair(q, o, 0, H)
        elif kind == EARLY_OWN:
            pass_pair(q, o, 0, F)

    def hop(d, kind):
        for way in (UP, DOWN):
            o = d if way == UP else NZ - d
            q = lax.rem(z + NZ - o, NZ)
            ref = ref_of(q, kind)
            arrived(ref, z_recv.at[way, d, kind])
            if d < 3:
                pass_z(ref, way, d + 1, kind)
            elif kind == HALF:
                pass_z(halves(q, way), way, d + 1, kind)
            elif kind == LATE and way in LATE_SIDES:
                pass_z(late_side(q, way), way, d + 1, kind)
            elif kind == (EARLY_OWN if way == UP else EARLY_OTHER):
                pass_z(ref, way, d + 1, kind)
            onward(q, o, kind)

    pl.semaphore_wait(barrier, len(peers))
    after = at_row(lax.rem(row + 1, ROWS))
    send(design_ref.at[here - taps : here, :], halo.at[taps : 2 * taps, :], halo_send.at[0], halo_recv.at[0], after)
    send(obs_own, halo_obs, halo_send.at[1], halo_recv.at[1], after)
    pass_parts(H)
    col_y(H)
    col_x(H)

    own, rows_f = filter_rows(0)
    early = three(jnp.where(own, rows_f, 0.0)[:, 0:mid])
    before = three(jnp.where(own, 0.0, rows_f)[:, here - 2 * taps :])
    arrived(halo.at[taps : 2 * taps, :], halo_recv.at[0])
    arrived(halo_obs, halo_recv.at[1])
    white = total(early, design_ref[0:mid, :]) + total(before, halo[...])
    cols[0:width, lanes_of(row, F)] = white.T.astype(jnp.bfloat16)
    obs_white = total_lanes(early, obs_own[:, 0:mid]) + total_lanes(before, halo_obs[:, here - 2 * taps :])
    cols[width : width + EXTRA, lanes_of(row, F)] = obs_white.astype(jnp.bfloat16)
    pass_parts(F)
    pass_rows(H)
    pass_rows(F)
    col_x(F)
    panel_arrived(H)
    pass_lo(piece(z, 0, H), 0)
    pass_z(ref_of(z, HALF), UP, 1, HALF)
    pass_z(ref_of(z, HALF), DOWN, 1, HALF)
    pass_pair(z, 0, 0, H)
    panel_arrived(F)
    pass_lo(early_rows(z, 0), NZ)
    for kind in (LATE, EARLY_OWN):
        pass_z(ref_of(z, kind), UP, 1, kind)
        pass_z(ref_of(z, kind), DOWN, 1, kind)
        onward(z, 0, kind)
    col_y(F)
    col_first(H)
    arrived(early_rows(z, 1), lo_recv.at[NZ])
    pass_z(early_rows(z, 1), UP, 1, EARLY_OTHER)
    pass_z(early_rows(z, 1), DOWN, 1, EARLY_OTHER)

    hop(1, HALF)
    hop(1, LATE)
    hop(1, EARLY_OWN)
    col_second(H)
    hop(1, EARLY_OTHER)
    col_first(F)
    lo_arrived(0)
    hop(2, HALF)
    lo_arrived(1)
    hop(2, LATE)
    hop(2, EARLY_OWN)
    lo_arrived(7)
    col_second(F)
    hop(2, EARLY_OTHER)
    hop(3, HALF)
    col_last(H)
    col_last(F)
    group(0)
    hop(3, LATE)
    group(1)
    hop(3, EARLY_OWN)
    lo_arrived(2)
    group(7)
    hop(3, EARLY_OTHER)
    lo_arrived(6)
    group(2)
    far = lax.rem(z + 4, NZ)
    for way in (UP, DOWN):
        arrived(halves(far, way), z_recv.at[way, 4, HALF])
    onward(far, 4, HALF)
    for way in LATE_SIDES:
        arrived(late_side(far, way), z_recv.at[way, 4, LATE])
    onward(far, 4, LATE)
    group(6)
    lo_arrived(3)
    lo_arrived(5)
    group(3)
    group(5)
    arrived(early_rows(far, 0), z_recv.at[UP, 4, EARLY_OWN])
    onward(far, 4, EARLY_OWN)
    arrived(early_rows(far, 1), z_recv.at[DOWN, 4, EARLY_OTHER])
    lo_arrived(4)
    group(4)

    for copy in started:
        copy.wait_send()
    for owner, away in conditional:

        @pl.when(owner != row)
        def _():
            away.wait_send()


def on_device(design, observations, filter_taps, tap_count, arc_id):
    here, width = design.shape
    taps, arcs = filter_taps.shape[0], tap_count.shape[0]
    deep = here * ROWS
    part = width // NZ
    vmem = pl.BlockSpec(memory_space=pltpu.VMEM)
    dma = pltpu.SemaphoreType.DMA
    bf16, f32 = jnp.bfloat16, jnp.float32
    whole = 16 * here

    def spread(value, start):
        return jnp.pad(value, (start, whole - start - value.shape[0])).astype(f32)

    table = spread(arc_id, 0) + spread(observations, deep) + spread(filter_taps, deep + here) + spread(tap_count, deep + 2 * here)
    done, cols, panel = pl.pallas_call(
        functools.partial(body, taps, arcs),
        out_shape=(
            jax.ShapeDtypeStruct((4, NZ, part, width), f32),
            jax.ShapeDtypeStruct((width + EXTRA, deep), bf16),
            jax.ShapeDtypeStruct((NZ, 4, part, deep), bf16),
        ),
        in_specs=[vmem, vmem],
        out_specs=(vmem, vmem, vmem),
        scratch_shapes=[
            pltpu.VMEM((2, NZ, part, here // 2), bf16),
            pltpu.VMEM((2 * taps, width), bf16),
            pltpu.VMEM((EXTRA, here), bf16),
            pltpu.VMEM((EXTRA, here), bf16),
            pltpu.VMEM((16, here), f32),
            dma((2,)), dma((2,)), dma((2, NZ)), dma((2, NZ)), dma((2, NZ)), dma((2, ROWS)),
            dma((2, 7)), dma((2, 7)), dma((2, 5, 4)), dma((2, 5, 4)), dma((17,)), dma((17,)),
            dma((NZ, 2, 2)), dma((NZ, 2, 2)),
        ],
        compiler_params=pltpu.CompilerParams(
            collective_id=0, has_side_effects=True, vmem_limit_bytes=LIMIT1 * 1024 * 1024
        ),
    )(design, table)
    normal, right = pl.pallas_call(
        finish,
        out_shape=(
            jax.ShapeDtypeStruct((4, NZ, part, width), f32),
            jax.ShapeDtypeStruct((width,), f32),
        ),
        in_specs=[vmem, vmem, vmem],
        out_specs=(pl.BlockSpec(memory_space=pl.ANY), vmem),
        scratch_shapes=[pltpu.VMEM((4, len(LATER), part, width), f32), dma((NZ,)), dma((3 * len(LATER),))],
        compiler_params=pltpu.CompilerParams(vmem_limit_bytes=LIMIT2 * 1024 * 1024),
    )(done, cols, panel)
    return normal.reshape(4 * width, width), right


def solution(mesh):
    finer = Mesh(mesh.devices.reshape(4, 2, 8, 2, 2), AXES)
    row, col = ("x", "yh"), ("z", "yl", "core")
    in_specs = (P(row, col), P(row), P(), P(), P())
    out_specs = (P(row, col), P(col))
    return jax.shard_map(
        on_device, mesh=finer, in_specs=in_specs, out_specs=out_specs, check_vma=False
    )
```

```python
import functools
import math

import jax
import jax.numpy as jnp
from jax import lax
from jax.experimental import pallas as pl
from jax.experimental.pallas import tpu as pltpu
from jax.sharding import Mesh
from jax.sharding import PartitionSpec as P

MESH = pl.DeviceIdType.MESH
LIMIT1, LIMIT2 = 28, 28
AXES = ("x", "yh", "z", "yl", "core")
NX, NZ = 4, 8
ROWS = 8
EXTRA = 16
UP, DOWN = 0, 1

LATER = (4,)
EARLY = 80
LATE_SIDES = (0,)
BY_LANE = (((1,), (1,)), ((), ()))


def multiply(panel, cols, out_ref, q, slot):
    _, lines, part, deep = panel.shape
    width = out_ref.shape[-1]
    tile = width // 3

    @pl.loop(0, 3)
    def _(n):
        lanes = pl.ds(pl.multiple_of(n * tile, tile), tile)
        result = lax.dot_general(
            panel[q].reshape(lines * part, deep), cols[lanes, :], BY_LANE, preferred_element_type=jnp.float32
        )
        out_ref[:, slot, :, lanes] = result.reshape(lines, part, tile) * (1.0 / deep)


def finish(done, cols, panel, out_ref, right_ref, last, sems, tile_sems):
    width = done.shape[-1]
    deep = panel.shape[-1]
    z = lax.axis_index("z")
    copies = []

    def write(source, q):
        copy = pltpu.make_async_copy(source, out_ref.at[:, q], sems.at[len(copies)])
        copy.start()
        copies.append(copy)

    for o in range(NZ):
        q = lax.rem(z + NZ - o, NZ)
        if o not in LATER:
            write(done.at[:, q], q)
    tiles = 3
    tile = width // tiles

    def tile_copy(t):
        slot, n = t // tiles, lax.rem(t, tiles)
        q = lax.rem(z + NZ - LATER[0] + slot, NZ)
        lanes = pl.ds(pl.multiple_of(n * tile, tile), tile)
        return q, slot, lanes, pltpu.make_async_copy(
            last.at[:, slot, :, lanes], out_ref.at[:, q, :, lanes], tile_sems.at[t]
        )

    @pl.loop(0, tiles * len(LATER))
    def _(t):
        q, slot, lanes, copy = tile_copy(t)
        result = lax.dot_general(
            panel[q].reshape(-1, deep), cols[lanes, :], BY_LANE, preferred_element_type=jnp.float32
        )
        last[:, slot, :, lanes] = result.reshape(last.shape[0], -1, tile) * (1.0 / deep)
        copy.start()

    right = lax.dot_general(cols[width:, :], cols[0:width, :], BY_LANE, preferred_element_type=jnp.float32)
    right_ref[...] = right[0:1, :].reshape(width) * (1.0 / math.sqrt(deep))
    for copy in copies:
        copy.wait()

    @pl.loop(0, tiles * len(LATER))
    def _(t):
        tile_copy(t)[3].wait()


def body(
    taps, arcs, design_ref, table_ref,
    out_ref, cols, panel,
    parts, halo, halo_obs, obs_own, table,
    halo_send, halo_recv, part_send, part_recv, panel_send, panel_recv,
    col_send, col_recv, z_send, z_recv, lo_send, lo_recv, pair_send, pair_recv,
):
    x, yh, z = lax.axis_index("x"), lax.axis_index("yh"), lax.axis_index("z")
    yl, core = lax.axis_index("yl"), lax.axis_index("core")
    row = x * 2 + yh
    mine = yl * 2 + core
    here, width = design_ref.shape
    part = width // NZ
    deep = here * ROWS
    half = deep // 2

    def at_row(r):
        return {"x": r // 2, "yh": lax.rem(r, 2)}

    barrier = pltpu.get_barrier_semaphore()
    peers = [at_row(lax.rem(row + i, ROWS)) for i in range(1, ROWS)]
    peers += [{"z": lax.rem(z + i, NZ)} for i in range(1, NZ)]
    peers += [{"yl": 1 - yl}, {"core": 1 - core}]
    for peer in peers:
        pl.semaphore_signal(barrier, inc=1, device_id=peer, device_id_type=MESH)

    table[...] = table_ref[...].reshape(table.shape)
    obs_own[...] = jnp.broadcast_to(table[ROWS : ROWS + 1, :], obs_own.shape).astype(jnp.bfloat16)
    halo[0:taps, :] = jnp.zeros((taps, width), jnp.bfloat16)

    started = []

    def send(src, dst, send_sem, recv_sem, device):
        copy = pltpu.make_async_remote_copy(
            src_ref=src, dst_ref=dst, send_sem=send_sem, recv_sem=recv_sem,
            device_id=device, device_id_type=MESH,
        )
        copy.start()
        started.append(copy)

    def arrived(dst, sem):
        pltpu.make_async_copy(dst, dst, sem).wait()

    mid = here // 2
    line = jnp.broadcast_to(table[ROWS + 1 : ROWS + 2, :], (here, here))
    shifted = pltpu.roll(line, 0, 1, stride=1, stride_axis=0)
    arc_here = table[pl.ds(row, 1), :]
    arc_before = jnp.where(row > 0, table[pl.ds(jnp.maximum(row - 1, 0), 1), :], -1.0)
    counts = jnp.zeros((1, here), jnp.float32)
    for a in range(arcs):
        counts = jnp.where(arc_here == a, table[ROWS + 2 : ROWS + 3, a : a + 1], counts)

    def filter_rows(start):
        shape = (mid, here)
        lag = lax.broadcasted_iota(jnp.int32, shape, 0) + start - lax.broadcasted_iota(jnp.int32, shape, 1)
        own = lag >= 0
        lag = jnp.where(own, lag, lag + here)
        arc_target = jnp.broadcast_to(arc_here[:, start : start + mid], (mid, mid)).T
        limit = jnp.broadcast_to(counts[:, start : start + mid], (mid, mid)).T
        arc_target = jnp.concatenate([arc_target, arc_target], axis=1)
        limit = jnp.concatenate([limit, limit], axis=1)
        arc_source = jnp.where(own, arc_here, arc_before)
        used = (arc_target == arc_source) & (lag.astype(jnp.float32) < limit) & (lag < taps)
        return own, jnp.where(used, shifted[:, start : start + mid].T, 0.0)

    def three(value):
        high = value.astype(jnp.bfloat16)
        rest = value - high.astype(jnp.float32)
        middle = rest.astype(jnp.bfloat16)
        return high, middle, (rest - middle.astype(jnp.float32)).astype(jnp.bfloat16)

    by_lane = (((1,), (1,)), ((), ()))

    def total(terms, value):
        return sum(jnp.dot(t, value, preferred_element_type=jnp.float32) for t in terms[::-1])

    def total_lanes(terms, value):
        return sum(
            lax.dot_general(value, t, by_lane, preferred_element_type=jnp.float32) for t in terms[::-1]
        )

    H, F = 0, 1

    def lanes_of(r, h):
        return pl.ds(pl.multiple_of(h * half + r * mid, mid), mid)

    late = three(filter_rows(mid)[1])
    cols[0:width, lanes_of(row, H)] = total(late, design_ref[...]).T.astype(jnp.bfloat16)
    cols[width : width + EXTRA, lanes_of(row, H)] = total_lanes(late, obs_own[...]).astype(jnp.bfloat16)
    def shard(r, h):
        return cols.at[:, lanes_of(r, h)]

    def own_part(q, h):
        return cols.at[pl.ds(pl.multiple_of(q * part, part), part), lanes_of(row, h)]

    right_x, left_x = lax.rem(x + 1, NX), lax.rem(x + NX - 1, NX)
    far_x = lax.rem(x + 2, NX)
    partner = x * 2 + 1 - yh
    near_first = [1, 7, 2, 6, 3, 5, 4]

    def pass_parts(h):
        for i in near_first[::-1]:
            q = lax.rem(z + i, NZ)
            send(own_part(q, h), parts.at[h, z], part_send.at[h, i], part_recv.at[h, i], {"z": q})

    def pass_col(r, h, slot, device):
        send(shard(r, h), shard(r, h), col_send.at[h, slot], col_recv.at[h, slot], device)

    def col_arrived(r, h, slot):
        arrived(shard(r, h), col_recv.at[h, slot])

    def col_y(h):
        pass_col(row, h, 0, {"yh": 1 - yh})

    def col_x(h):
        pass_col(row, h, 1, {"x": right_x})
        pass_col(row, h, 2, {"x": left_x})

    def col_first(h):
        col_arrived(partner, h, 0)
        pass_col(partner, h, 3, {"x": right_x})
        pass_col(partner, h, 4, {"x": left_x})
        col_arrived(left_x * 2 + yh, h, 1)
        pass_col(left_x * 2 + yh, h, 5, {"x": right_x})

    def col_second(h):
        col_arrived(right_x * 2 + 1 - yh, h, 4)
        pass_col(right_x * 2 + 1 - yh, h, 6, {"x": left_x})

    def col_last(h):
        col_arrived(left_x * 2 + 1 - yh, h, 3)
        col_arrived(right_x * 2 + yh, h, 2)
        col_arrived(far_x * 2 + yh, h, 5)
        col_arrived(far_x * 2 + 1 - yh, h, 6)

    conditional = []

    def pass_rows(h):
        for i in [0] + near_first:
            owner = lax.rem(z + NZ - i, NZ)
            source = parts.at[h, owner]
            if i == 0:
                source = own_part(z, h)
            else:
                arrived(source, part_recv.at[h, i])
            target_ref = panel.at[z, mine, :, lanes_of(row, h)]
            away = pltpu.make_async_remote_copy(
                src_ref=source, dst_ref=target_ref, send_sem=panel_send.at[h, i],
                recv_sem=panel_recv.at[h, row], device_id=at_row(owner), device_id_type=MESH,
            )
            local = pltpu.make_async_copy(source, target_ref, panel_recv.at[h, row])

            @pl.when(owner != row)
            def _():
                away.start()

            @pl.when(owner == row)
            def _():
                local.start()

            conditional.append((owner, away))

    above, below = {"z": lax.rem(z + 1, NZ)}, {"z": lax.rem(z + NZ - 1, NZ)}
    z_device = (above, below)

    def piece(q, other, h, other_core=False):
        line_of = 1 - yl if other else yl
        core_of = 1 - core if other_core else core
        return panel.at[q, line_of * 2 + core_of, :, h * half : (h + 1) * half]

    def halves(q, side):
        return panel.at[q, mine, side * (part // 2) : (side + 1) * (part // 2), 0:half]

    def early_rows(q, other):
        line_of = 1 - yl if other else yl
        return panel.at[q, line_of * 2 + core, 0:EARLY, half:deep]

    def late_rows(q, other):
        line_of = 1 - yl if other else yl
        return panel.at[q, line_of * 2 + core, EARLY:part, half:deep]

    def late_side(q, side):
        cut = EARLY + (part - EARLY) // 2 if len(LATE_SIDES) == 2 else part
        start, stop = (EARLY, cut) if side == UP else (cut, part)
        return panel.at[q, mine, start:stop, half:deep]

    def pass_z(ref, way, d, kind):
        send(ref, ref, z_send.at[way, d, kind], z_recv.at[way, d, kind], z_device[way])

    def pass_lo(ref, slot):
        send(ref, ref, lo_send.at[slot], lo_recv.at[slot], {"yl": 1 - yl})

    def pass_pair(q, o, other, h):
        ref = piece(q, other, h)
        send(ref, ref, pair_send.at[o, other, h], pair_recv.at[o, other, h], {"core": 1 - core})

    def panel_arrived(h):
        for e in range(ROWS):
            start = h * half + e * mid
            arrived(panel.at[z, mine, :, start : start + mid], panel_recv.at[h, e])

    def group(o):
        q = lax.rem(z + NZ - o, NZ)
        for other in (0, 1):
            for h in (F, H):
                arrived(piece(q, other, h, True), pair_recv.at[o, other, h])
        if o not in LATER:
            multiply(panel, cols, out_ref, q, q)

    def lo_arrived(o):
        q = lax.rem(z + NZ - o, NZ)
        arrived(piece(q, 1, H), lo_recv.at[o])
        pass_pair(q, o, 1, H)
        arrived(late_rows(q, 1), lo_recv.at[NZ + 1 + o])
        pass_pair(q, o, 1, F)

    EARLY_OWN, LATE, HALF, EARLY_OTHER = 0, 1, 2, 3

    def ref_of(q, kind):
        if kind == EARLY_OWN:
            return early_rows(q, 0)
        if kind == LATE:
            return late_rows(q, 0)
        if kind == HALF:
            return piece(q, 0, H)
        return early_rows(q, 1)

    def onward(q, o, kind):
        if kind == LATE:
            pass_lo(late_rows(q, 0), NZ + 1 + o)
        elif kind == HALF:
            pass_lo(piece(q, 0, H), o)
            pass_pair(q, o, 0, H)
        elif kind == EARLY_OWN:
            pass_pair(q, o, 0, F)

    def hop(d, kind):
        for way in (UP, DOWN):
            o = d if way == UP else NZ - d
            q = lax.rem(z + NZ - o, NZ)
            ref = ref_of(q, kind)
            arrived(ref, z_recv.at[way, d, kind])
            if d < 3:
                pass_z(ref, way, d + 1, kind)
            elif kind == HALF:
                pass_z(halves(q, way), way, d + 1, kind)
            elif kind == LATE and way in LATE_SIDES:
                pass_z(late_side(q, way), way, d + 1, kind)
            elif kind == (EARLY_OWN if way == UP else EARLY_OTHER):
                pass_z(ref, way, d + 1, kind)
            onward(q, o, kind)

    pl.semaphore_wait(barrier, len(peers))
    after = at_row(lax.rem(row + 1, ROWS))
    send(design_ref.at[here - taps : here, :], halo.at[taps : 2 * taps, :], halo_send.at[0], halo_recv.at[0], after)
    send(obs_own, halo_obs, halo_send.at[1], halo_recv.at[1], after)
    pass_parts(H)
    col_y(H)
    col_x(H)

    own, rows_f = filter_rows(0)
    early = three(jnp.where(own, rows_f, 0.0)[:, 0:mid])
    before = three(jnp.where(own, 0.0, rows_f)[:, here - 2 * taps :])
    arrived(halo.at[taps : 2 * taps, :], halo_recv.at[0])
    arrived(halo_obs, halo_recv.at[1])
    white = total(early, design_ref[0:mid, :]) + total(before, halo[...])
    cols[0:width, lanes_of(row, F)] = white.T.astype(jnp.bfloat16)
    obs_white = total_lanes(early, obs_own[:, 0:mid]) + total_lanes(before, halo_obs[:, here - 2 * taps :])
    cols[width : width + EXTRA, lanes_of(row, F)] = obs_white.astype(jnp.bfloat16)
    pass_parts(F)
    pass_rows(H)
    pass_rows(F)
    col_x(F)
    panel_arrived(H)
    pass_lo(piece(z, 0, H), 0)
    pass_z(ref_of(z, HALF), UP, 1, HALF)
    pass_z(ref_of(z, HALF), DOWN, 1, HALF)
    pass_pair(z, 0, 0, H)
    panel_arrived(F)
    pass_lo(early_rows(z, 0), NZ)
    for kind in (LATE, EARLY_OWN):
        pass_z(ref_of(z, kind), UP, 1, kind)
        pass_z(ref_of(z, kind), DOWN, 1, kind)
        onward(z, 0, kind)
    col_y(F)
    col_first(H)
    arrived(early_rows(z, 1), lo_recv.at[NZ])
    pass_z(early_rows(z, 1), UP, 1, EARLY_OTHER)
    pass_z(early_rows(z, 1), DOWN, 1, EARLY_OTHER)

    hop(1, HALF)
    hop(1, LATE)
    hop(1, EARLY_OWN)
    col_second(H)
    hop(1, EARLY_OTHER)
    col_first(F)
    lo_arrived(0)
    hop(2, HALF)
    lo_arrived(1)
    hop(2, LATE)
    hop(2, EARLY_OWN)
    lo_arrived(7)
    col_second(F)
    hop(2, EARLY_OTHER)
    hop(3, HALF)
    col_last(H)
    col_last(F)
    group(0)
    hop(3, LATE)
    group(1)
    hop(3, EARLY_OWN)
    lo_arrived(2)
    group(7)
    hop(3, EARLY_OTHER)
    lo_arrived(6)
    group(2)
    group(6)
    far = lax.rem(z + 4, NZ)
    for way in (UP, DOWN):
        arrived(halves(far, way), z_recv.at[way, 4, HALF])
    onward(far, 4, HALF)
    for way in LATE_SIDES:
        arrived(late_side(far, way), z_recv.at[way, 4, LATE])
    onward(far, 4, LATE)
    lo_arrived(3)
    lo_arrived(5)
    group(3)
    group(5)
    arrived(early_rows(far, 0), z_recv.at[UP, 4, EARLY_OWN])
    onward(far, 4, EARLY_OWN)
    arrived(early_rows(far, 1), z_recv.at[DOWN, 4, EARLY_OTHER])
    lo_arrived(4)
    group(4)

    for copy in started:
        copy.wait_send()
    for owner, away in conditional:

        @pl.when(owner != row)
        def _():
            away.wait_send()


def on_device(design, observations, filter_taps, tap_count, arc_id):
    here, width = design.shape
    taps, arcs = filter_taps.shape[0], tap_count.shape[0]
    deep = here * ROWS
    part = width // NZ
    vmem = pl.BlockSpec(memory_space=pltpu.VMEM)
    dma = pltpu.SemaphoreType.DMA
    bf16, f32 = jnp.bfloat16, jnp.float32
    whole = 16 * here

    def spread(value, start):
        return jnp.pad(value, (start, whole - start - value.shape[0])).astype(f32)

    table = spread(arc_id, 0) + spread(observations, deep) + spread(filter_taps, deep + here) + spread(tap_count, deep + 2 * here)
    done, cols, panel = pl.pallas_call(
        functools.partial(body, taps, arcs),
        out_shape=(
            jax.ShapeDtypeStruct((4, NZ, part, width), f32),
            jax.ShapeDtypeStruct((width + EXTRA, deep), bf16),
            jax.ShapeDtypeStruct((NZ, 4, part, deep), bf16),
        ),
        in_specs=[vmem, vmem],
        out_specs=(vmem, vmem, vmem),
        scratch_shapes=[
            pltpu.VMEM((2, NZ, part, here // 2), bf16),
            pltpu.VMEM((2 * taps, width), bf16),
            pltpu.VMEM((EXTRA, here), bf16),
            pltpu.VMEM((EXTRA, here), bf16),
            pltpu.VMEM((16, here), f32),
            dma((2,)), dma((2,)), dma((2, NZ)), dma((2, NZ)), dma((2, NZ)), dma((2, ROWS)),
            dma((2, 7)), dma((2, 7)), dma((2, 5, 4)), dma((2, 5, 4)), dma((17,)), dma((17,)),
            dma((NZ, 2, 2)), dma((NZ, 2, 2)),
        ],
        compiler_params=pltpu.CompilerParams(
            collective_id=0, has_side_effects=True, vmem_limit_bytes=LIMIT1 * 1024 * 1024
        ),
    )(design, table)
    normal, right = pl.pallas_call(
        finish,
        out_shape=(
            jax.ShapeDtypeStruct((4, NZ, part, width), f32),
            jax.ShapeDtypeStruct((width,), f32),
        ),
        in_specs=[vmem, vmem, vmem],
        out_specs=(pl.BlockSpec(memory_space=pl.ANY), vmem),
        scratch_shapes=[pltpu.VMEM((4, len(LATER), part, width), f32), dma((NZ,)), dma((3 * len(LATER),))],
        compiler_params=pltpu.CompilerParams(vmem_limit_bytes=LIMIT2 * 1024 * 1024),
    )(done, cols, panel)
    return normal.reshape(4 * width, width), right


def solution(mesh):
    finer = Mesh(mesh.devices.reshape(4, 2, 8, 2, 2), AXES)
    row, col = ("x", "yh"), ("z", "yl", "core")
    in_specs = (P(row, col), P(row), P(), P(), P())
    out_specs = (P(row, col), P(col))
    return jax.shard_map(
        on_device, mesh=finer, in_specs=in_specs, out_specs=out_specs, check_vma=False
    )
```
